32 devices in a mesh: ctx: 2 (over y), branch: 4 (over z), head: 4 (over x, core).
Axes of the slice: x: 2, y: 2, z: 4, core: 2. Of those that a mesh axis runs over, the one named last changes fastest.
Arguments:
- queries: bfloat16 [8, 128, 4096], P(('ctx', 'branch'), None, 'head'), may hold values from -320 to 320
- branch_keys: bfloat16 [8, 128, 512], P(('ctx', 'branch'), None, 'head'), may hold values from -12 to 12
- branch_value_rows: bfloat16 [8, 128, 512], P(('ctx', 'branch'), None, 'head'), may hold values from -6 to 6
- trunk_key_rows: bfloat16 [192, 512], P('ctx', 'head'), may hold values from -6 to 6
- trunk_value_rows: bfloat16 [192, 512], P('ctx', 'head'), may hold values from -6 to 6
- attn_out: bfloat16 [8, 128, 4096], P(('ctx', 'branch'), None, 'head'), may hold values from -2 to 2
- out_grad: bfloat16 [8, 128, 4096], P(('ctx', 'branch'), None, 'head'), may hold values from -6 to 6
- block_mask: int32 [8, 1, 3], P(('ctx', 'branch')), may hold values from 0 to 1, as said below
Outputs:
- query_grad: bfloat16 [8, 128, 4096], P(('ctx', 'branch'), None, 'head')
- branch_kv_grad: bfloat16 [8, 128, 1024], P(('ctx', 'branch'), None, 'head')
- trunk_kv_grad: bfloat16 [192, 1024], P(('ctx', 'branch'), 'head')
The draws below stay inside these ranges and needn't reach their ends.
Inputs may be any that keep to these rules, and one draw needn't show every extreme that they name: `block_mask`: each entry is 0 or 1; columns 0 to 1 are the trunk's blocks, the rest the branch's own blocks, of which those on or above the query block's diagonal are not read. Every query block of every branch sees at least one trunk block. The share of ones differs from branch to branch.
All inputs are finite; a program needn't handle non-finite values.
Results may differ from the reference program's by a relative error of at most 0.017.
Values may be sent and summed in bfloat16 or wider, within the bound.
No kernel may reach another device: no remote copies, remote signals or barrier semaphores. Data moves between devices by JAX's collectives and lax.ppermute only.
A program may use at most 64 MiB of HBM per device.

```python
import math
import jax
import jax.numpy as jnp
from jax import lax

HEAD_WIDTH = 128
QUERY_HEADS = 32
KEY_VALUE_HEADS = 4
BLK = 128
BRANCH_LENGTH = 128
BRANCH_COUNT = 8
TRUNK_TOKENS = 192
QB = 1
TB = 2


def drawn_draw(key):
    base_key = jax.random.fold_in(key, 17)
    key_portion, query_portion = jax.random.split(base_key, 2)
    group_width = QUERY_HEADS // KEY_VALUE_HEADS
    key_row_block = jnp.clip(jax.random.normal(key_portion, (BRANCH_COUNT, BRANCH_LENGTH, KEY_VALUE_HEADS, HEAD_WIDTH), jnp.float32), -4.0, 4.0)
    query_row_block = jnp.clip(jax.random.normal(query_portion, (BRANCH_COUNT, BRANCH_LENGTH, KEY_VALUE_HEADS, group_width, HEAD_WIDTH), jnp.float32), -4.0, 4.0)
    return (key_row_block.reshape(BRANCH_COUNT, BRANCH_LENGTH, KEY_VALUE_HEADS * HEAD_WIDTH), query_row_block.reshape(BRANCH_COUNT, BRANCH_LENGTH, QUERY_HEADS * HEAD_WIDTH))


def draw_queries(key, part):
    return drawn_draw(key)[1].astype(jnp.bfloat16)


def draw_branch_keys(key, part):
    return drawn_draw(key)[0].astype(jnp.bfloat16)


def draw_block_mask(key, part):
    base_key = jax.random.fold_in(key, 29)
    level_key, cell_key, column_key = jax.random.split(base_key, 3)
    levels = jax.random.randint(level_key, (BRANCH_COUNT, 1, 1), 2, 9)
    random_cells = jax.random.randint(cell_key, (BRANCH_COUNT, QB, TB + QB), 0, 16)
    forced_column = jax.random.randint(column_key, (BRANCH_COUNT, QB, 1), 0, TB)
    columns = jnp.arange(TB + QB, dtype=jnp.int32)[None, None, :]
    return ((random_cells < levels) | (columns == forced_column)).astype(jnp.int32)


def shard_levels(rng, dims, shards, low, largest):
    loudness = 1.0
    for dim, blocks in shards:
        steps = jax.random.uniform(jax.random.fold_in(jax.random.fold_in(rng, 6), dim), (blocks,), jnp.float32, low / len(shards), largest / len(shards))
        loudness = loudness * jnp.repeat(jnp.exp(steps), dims[dim] // blocks).reshape((-1,) + (1,) * (len(dims) - 1 - dim))
    return loudness


def bell_draw(rng, shape, deviation, most, cuts=(), kind=jnp.bfloat16):
    values = jax.random.normal(rng, shape, jnp.float32) * deviation
    if len(cuts) > 0:
        values = shard_levels(rng, shape, cuts, -0.22, 0.18) * values
    return jnp.clip(values, min=-most, max=most).astype(kind)


def setup_inputs(seed: int = 0) -> dict:
    streams_of = jax.random.split(jax.random.key(seed), 9)
    return {
        "queries": draw_queries(jax.random.fold_in(streams_of[8], 71), 0),
        "branch_keys": draw_branch_keys(jax.random.fold_in(streams_of[8], 71), 0),
        "branch_value_rows": bell_draw(streams_of[2], (BRANCH_COUNT, BRANCH_LENGTH, KEY_VALUE_HEADS * HEAD_WIDTH), 1.0, 6.0, ((0, 8), (2, 4))),
        "trunk_key_rows": bell_draw(streams_of[3], (TRUNK_TOKENS, KEY_VALUE_HEADS * HEAD_WIDTH), 1.0, 6.0, ((0, 2), (1, 4))),
        "trunk_value_rows": bell_draw(streams_of[4], (TRUNK_TOKENS, KEY_VALUE_HEADS * HEAD_WIDTH), 1.0, 6.0, ((0, 2), (1, 4))),
        "attn_out": bell_draw(streams_of[5], (BRANCH_COUNT, BRANCH_LENGTH, QUERY_HEADS * HEAD_WIDTH), 0.3, 2.0, ((0, 8), (2, 4))),
        "out_grad": bell_draw(streams_of[6], (BRANCH_COUNT, BRANCH_LENGTH, QUERY_HEADS * HEAD_WIDTH), 1.0, 6.0, ((0, 8), (2, 4))),
        "block_mask": draw_block_mask(jax.random.fold_in(streams_of[8], 71), 0),
    }


masked_fill = -1e+30

def rounded(values):
    return lax.optimization_barrier(values.astype(jnp.bfloat16)).astype(jnp.float32)

def allowed_keys(mask_rows):
    position = jnp.arange(BRANCH_LENGTH, dtype=jnp.int32)
    query_block = position // BLK
    trunk_block = jnp.arange(TRUNK_TOKENS, dtype=jnp.int32) // BLK
    trunk_part = mask_rows[query_block[:, None], trunk_block[None, :]] == 1
    own_mask = mask_rows[query_block[:, None], TB + query_block[None, :]] == 1
    earlier = (query_block[None, :] < query_block[:, None]) & own_mask
    causal = (query_block[None, :] == query_block[:, None]) & (position[None, :] <= position[:, None])
    return jnp.concatenate([trunk_part, earlier | causal], axis=1)

def branch_grads(query_row_block, branch_own_keys, branch_own_values, trunk_key_rows, trunk_value_rows, output_rows, gradient_rows, mask_rows):
    group_width = QUERY_HEADS // KEY_VALUE_HEADS
    score_scale = 1.0 / math.sqrt(HEAD_WIDTH)
    query_head_rows = query_row_block.reshape(BRANCH_LENGTH, KEY_VALUE_HEADS, group_width, HEAD_WIDTH).astype(jnp.float32)
    gradient_heads = gradient_rows.reshape(BRANCH_LENGTH, KEY_VALUE_HEADS, group_width, HEAD_WIDTH).astype(jnp.float32)
    output_heads = output_rows.reshape(BRANCH_LENGTH, KEY_VALUE_HEADS, group_width, HEAD_WIDTH).astype(jnp.float32)
    key_matrix = jnp.concatenate([trunk_key_rows, branch_own_keys], axis=0).reshape(TRUNK_TOKENS + BRANCH_LENGTH, KEY_VALUE_HEADS, HEAD_WIDTH).astype(jnp.float32)
    value_matrix = jnp.concatenate([trunk_value_rows, branch_own_values], axis=0).reshape(TRUNK_TOKENS + BRANCH_LENGTH, KEY_VALUE_HEADS, HEAD_WIDTH).astype(jnp.float32)
    allowed = allowed_keys(mask_rows)[None, None]
    scores = jnp.einsum('ihgd,khd->hgik', query_head_rows, key_matrix) * score_scale
    masked = jnp.where(allowed, scores, masked_fill)
    row_max = lax.optimization_barrier(jnp.max(masked, axis=3, keepdims=True))
    log_total = row_max + jnp.log(lax.optimization_barrier(jnp.sum(jnp.exp(masked - row_max), axis=3, keepdims=True)))
    weights = jnp.exp(masked - log_total)
    weights_low = rounded(weights)
    out_dot = jnp.transpose(lax.optimization_barrier(jnp.sum(gradient_heads * output_heads, axis=3)), (1, 2, 0))[..., None]
    grad_weights = jnp.einsum('ihgd,khd->hgik', gradient_heads, value_matrix)
    grad_scores = rounded(weights * (grad_weights - out_dot))
    query_grad = jnp.einsum('hgik,khd->ihgd', grad_scores, key_matrix) * score_scale
    key_gradient = jnp.einsum('hgik,ihgd->khd', grad_scores, query_head_rows) * score_scale
    value_gradient = jnp.einsum('hgik,ihgd->khd', weights_low, gradient_heads)
    key_value_pair = jnp.concatenate([key_gradient, value_gradient], axis=2).reshape(TRUNK_TOKENS + BRANCH_LENGTH, KEY_VALUE_HEADS * 2 * HEAD_WIDTH)
    query_out = query_grad.reshape(BRANCH_LENGTH, QUERY_HEADS * HEAD_WIDTH).astype(jnp.bfloat16)
    return (query_out, key_value_pair[TRUNK_TOKENS:].astype(jnp.bfloat16), rounded(key_value_pair[:TRUNK_TOKENS]))

def reference(queries, branch_keys, branch_value_rows, trunk_key_rows, trunk_value_rows, attn_out, out_grad, block_mask):

    def advance(running_sum, inputs):
        query_row_block, branch_own_keys, branch_own_values, output_rows, gradient_rows, mask_rows = inputs
        query_out, branch_out, trunk_term = branch_grads(query_row_block, branch_own_keys, branch_own_values, trunk_key_rows, trunk_value_rows, output_rows, gradient_rows, mask_rows)
        return (running_sum + trunk_term, (query_out, branch_out))
    initial_sum = jnp.zeros((TRUNK_TOKENS, KEY_VALUE_HEADS * 2 * HEAD_WIDTH), jnp.float32)
    trunk_sum, outputs = lax.scan(advance, initial_sum, (queries, branch_keys, branch_value_rows, attn_out, out_grad, block_mask))
    return (outputs[0], outputs[1], trunk_sum.astype(jnp.bfloat16))
```

```python
import functools
import math

import jax
import jax.numpy as jnp
from jax import lax
from jax.experimental import pallas as pl
from jax.experimental.pallas import tpu as pltpu
from jax.sharding import PartitionSpec as P

HEAD_WIDTH = 128
BLK = 128


masked_fill = -1e30
VMEM = pl.BlockSpec(memory_space=pltpu.VMEM)
SMEM = pl.BlockSpec(memory_space=pltpu.SMEM)
NT = (((1,), (1,)), ((), ()))
TN = (((0,), (0,)), ((), ()))


def mm(a, b, dims=(((1,), (0,)), ((), ()))):
    return lax.dot_general(a, b, dims, preferred_element_type=jnp.float32)


def stacked(ref, chunk, heads):
    return jnp.concatenate(
        [
            ref[0, :, j * HEAD_WIDTH : (j + 1) * HEAD_WIDTH]
            for j in range(chunk * heads, (chunk + 1) * heads)
        ],
        axis=0,
    )


def trunk_visible(mask_ref, part_ref, shape, trunk_blocks):
    token = part_ref[0] * shape[0] + lax.broadcasted_iota(jnp.int32, shape, 0)
    visible = jnp.zeros(shape, jnp.int32)
    for block in range(trunk_blocks):
        inside = (token >= block * BLK) & (token < (block + 1) * BLK)
        visible = jnp.where(inside, mask_ref[0, 0, block], visible)
    return visible > 0


def own_kernel(
    trunk_blocks,
    heads,
    mask_ref,
    part_ref,
    q_ref,
    g_ref,
    o_ref,
    bk_ref,
    bv_ref,
    tk_ref,
    tv_ref,
    e_ref,
    gs_ref,
    stat_ref,
):
    rows = q_ref.shape[1]
    own = bk_ref.shape[1]
    scale = 1.0 / math.sqrt(HEAD_WIDTH)
    keys = jnp.concatenate([bk_ref[0], tk_ref[...]], axis=0)
    values = jnp.concatenate([bv_ref[0], tv_ref[...]], axis=0)
    width = heads * rows
    key_row = lax.broadcasted_iota(jnp.int32, (own, rows), 0)
    query_row = lax.broadcasted_iota(jnp.int32, (own, rows), 1)
    causal = key_row <= query_row
    visible = trunk_visible(mask_ref, part_ref, (tk_ref.shape[0], rows), trunk_blocks)
    allowed = jnp.concatenate([jnp.concatenate([causal, visible], axis=0)] * heads, axis=1)
    ones = jnp.ones((8, HEAD_WIDTH), jnp.bfloat16)
    for chunk in range(q_ref.shape[2] // (heads * HEAD_WIDTH)):
        at = slice(chunk * width, (chunk + 1) * width)
        q = stacked(q_ref, chunk, heads)
        g = stacked(g_ref, chunk, heads)
        prod = g.astype(jnp.float32) * stacked(o_ref, chunk, heads).astype(jnp.float32)
        high = prod.astype(jnp.bfloat16)
        low = (prod - high.astype(jnp.float32)).astype(jnp.bfloat16)
        dot = mm(ones, high, NT) + mm(ones, low, NT)
        s = jnp.where(allowed, mm(keys, q, NT) * scale, masked_fill)
        top = jnp.max(s, axis=0, keepdims=True)
        e = jnp.exp(s - top)
        e_ref[:, at] = e
        gs_ref[:, at] = e * (mm(values, g, NT) - dot[:1])
        stat_ref[0:8, at] = jnp.broadcast_to(top, (8, width))
        stat_ref[8:16, at] = jnp.broadcast_to(jnp.sum(e, axis=0, keepdims=True), (8, width))
        stat_ref[16:24, at] = dot


def far_kernel(
    trunk_blocks,
    heads,
    mask_ref,
    part_ref,
    q_ref,
    g_ref,
    kv_ref,
    stat_ref,
    pair_ref,
    ds_ref,
    factor_ref,
):
    rows = q_ref.shape[1]
    count = kv_ref.shape[0] // 2
    scale = 1.0 / math.sqrt(HEAD_WIDTH)
    keys = kv_ref[:count]
    values = kv_ref[count:]
    width = heads * rows
    visible = trunk_visible(mask_ref, part_ref, (count, rows), trunk_blocks)
    visible = jnp.concatenate([visible] * heads, axis=1)
    dk = jnp.zeros((count, HEAD_WIDTH), jnp.float32)
    dv = jnp.zeros((count, HEAD_WIDTH), jnp.float32)
    for chunk in range(q_ref.shape[2] // (heads * HEAD_WIDTH)):
        at = slice(chunk * width, (chunk + 1) * width)
        q = stacked(q_ref, chunk, heads)
        g = stacked(g_ref, chunk, heads)
        s = jnp.where(visible, mm(keys, q, NT) * scale, masked_fill)
        old = stat_ref[0:1, at]
        top = jnp.maximum(old, jnp.max(s, axis=0, keepdims=True))
        e = jnp.exp(s - top)
        shrink = jnp.exp(old - top)
        total = stat_ref[8:9, at] * shrink + jnp.sum(e, axis=0, keepdims=True)
        inverse = 1.0 / total
        w = e * inverse
        ds = (w * (mm(values, g, NT) - stat_ref[16:17, at])).astype(jnp.bfloat16)
        dk += mm(ds, q)
        dv += mm(w.astype(jnp.bfloat16), g)
        ds_ref[:, at] = ds
        factor_ref[:, at] = jnp.broadcast_to(shrink * inverse, (8, width))
    pair_ref[:, :HEAD_WIDTH] = (dk * scale).astype(jnp.bfloat16)
    pair_ref[:, HEAD_WIDTH:] = dv.astype(jnp.bfloat16)


def rest_kernel(
    heads,
    q_ref,
    g_ref,
    bk_ref,
    tk_ref,
    kv_ref,
    e_ref,
    gs_ref,
    ds_ref,
    factor_ref,
    dq_ref,
    branch_ref,
    trunk_ref,
):
    rows = q_ref.shape[1]
    own = bk_ref.shape[1]
    count = tk_ref.shape[0]
    scale = 1.0 / math.sqrt(HEAD_WIDTH)
    keys = jnp.concatenate([bk_ref[0], tk_ref[...], kv_ref[:count]], axis=0)
    width = heads * rows
    dk = jnp.zeros((own + count, HEAD_WIDTH), jnp.float32)
    dv = jnp.zeros((own + count, HEAD_WIDTH), jnp.float32)
    for chunk in range(q_ref.shape[2] // (heads * HEAD_WIDTH)):
        at = slice(chunk * width, (chunk + 1) * width)
        q = stacked(q_ref, chunk, heads)
        g = stacked(g_ref, chunk, heads)
        factor = factor_ref[0:1, at]
        w = (e_ref[:, at] * factor).astype(jnp.bfloat16)
        ds = (gs_ref[:, at] * factor).astype(jnp.bfloat16)
        dk += mm(ds, q)
        dv += mm(w, g)
        dq = mm(keys, jnp.concatenate([ds, ds_ref[:, at]], axis=0), TN) * scale
        for j in range(heads):
            head = chunk * heads + j
            dq_ref[0, :, head * HEAD_WIDTH : (head + 1) * HEAD_WIDTH] = (
                dq[:, j * rows : (j + 1) * rows].T.astype(jnp.bfloat16)
            )
    dk = (dk * scale).astype(jnp.bfloat16)
    dv = dv.astype(jnp.bfloat16)
    branch_ref[0, :, :HEAD_WIDTH] = dk[:own]
    branch_ref[0, :, HEAD_WIDTH:] = dv[:own]
    trunk_ref[:, :HEAD_WIDTH] = dk[own:]
    trunk_ref[:, HEAD_WIDTH:] = dv[own:]


def call(kernel, out_shape, in_specs, flops, bytes_accessed):
    return pl.pallas_call(
        kernel,
        out_shape=out_shape,
        in_specs=in_specs,
        out_specs=[VMEM] * len(out_shape),
        cost_estimate=pl.CostEstimate(
            flops=flops, bytes_accessed=bytes_accessed, transcendentals=0
        ),
        compiler_params=pltpu.CompilerParams(vmem_limit_bytes=16 << 20),
    )


def halved(rows, axis, bit):
    size = lax.axis_size(axis)
    mine = (lax.axis_index(axis) // bit) % 2
    parts = rows.reshape(2, rows.shape[0] // 2, rows.shape[1])
    other = lax.ppermute(
        lax.dynamic_index_in_dim(parts, 1 - mine, 0, False),
        axis,
        [(i, i ^ bit) for i in range(size)],
    )
    kept = lax.dynamic_index_in_dim(parts, mine, 0, False)
    return (kept.astype(jnp.float32) + other.astype(jnp.float32)).astype(jnp.bfloat16)


def paired_shards(
    queries,
    branch_keys,
    branch_value_rows,
    trunk_key_rows,
    trunk_value_rows,
    attn_out,
    out_grad,
    block_mask,
):
    rows = queries.shape[1]
    group = queries.shape[2] // HEAD_WIDTH
    own = branch_keys.shape[1]
    count = trunk_key_rows.shape[0]
    trunk_blocks = block_mask.shape[2] - rows // BLK
    heads = 2 if group % 2 == 0 else 1
    lanes = group * rows
    swap = [(0, 1), (1, 0)]
    near_part = lax.axis_index("ctx").astype(jnp.int32).reshape(1)
    far_part = 1 - near_part
    far = lax.ppermute(jnp.concatenate([trunk_key_rows, trunk_value_rows], axis=0), "ctx", swap)
    near = own + count
    mac = 2 * lanes * HEAD_WIDTH
    shape = jax.ShapeDtypeStruct
    e, gs, stats = call(
        functools.partial(own_kernel, trunk_blocks, heads),
        [
            shape((near, lanes), jnp.float32),
            shape((near, lanes), jnp.float32),
            shape((24, lanes), jnp.float32),
        ],
        [SMEM, SMEM] + [VMEM] * 7,
        2 * near * mac,
        6 * rows * lanes,
    )(
        block_mask,
        near_part,
        queries,
        out_grad,
        attn_out,
        branch_keys,
        branch_value_rows,
        trunk_key_rows,
        trunk_value_rows,
    )
    pair, ds, factor = call(
        functools.partial(far_kernel, trunk_blocks, heads),
        [
            shape((count, 2 * HEAD_WIDTH), jnp.bfloat16),
            shape((count, lanes), jnp.bfloat16),
            shape((8, lanes), jnp.float32),
        ],
        [SMEM, SMEM] + [VMEM] * 4,
        4 * count * mac,
        4 * rows * lanes,
    )(block_mask, far_part, queries, out_grad, far, stats)
    came = lax.ppermute(pair, "ctx", swap)
    query_out, branch_out, kept = call(
        functools.partial(rest_kernel, heads),
        [
            shape(queries.shape, jnp.bfloat16),
            shape((1, own, 2 * HEAD_WIDTH), jnp.bfloat16),
            shape((count, 2 * HEAD_WIDTH), jnp.bfloat16),
        ],
        [VMEM] * 9,
        (2 * near + near + count) * mac,
        6 * rows * lanes,
    )(queries, out_grad, branch_keys, trunk_key_rows, far, e, gs, ds, factor)
    total = (kept.astype(jnp.float32) + came.astype(jnp.float32)).astype(jnp.bfloat16)
    bit = lax.axis_size("branch") // 2
    while bit:
        total = halved(total, "branch", bit)
        bit //= 2
    return (query_out, branch_out, total)


def head_scores(query_row_block, key_row_block, score_scale):
    return (
        jnp.einsum(
            "igd,kd->gik", query_row_block, key_row_block, preferred_element_type=jnp.float32
        )
        * score_scale
    )
def block_gradients(
    query_row_block,
    gradient_rows,
    key_row_block,
    value_rows,
    allowed,
    log_total,
    out_dot,
    score_scale,
):
    scores = head_scores(query_row_block, key_row_block, score_scale)
    weights = jnp.exp(jnp.where(allowed[None], scores, masked_fill) - log_total)
    weights_low = weights.astype(jnp.bfloat16)
    grad_weights = jnp.einsum(
        "igd,kd->gik", gradient_rows, value_rows, preferred_element_type=jnp.float32
    )
    grad_scores = (weights * (grad_weights - out_dot)).astype(jnp.bfloat16)
    query_portion = jnp.einsum(
        "gik,kd->igd", grad_scores, key_row_block, preferred_element_type=jnp.float32
    )
    key_gradient = (
        jnp.einsum("gik,igd->kd", grad_scores, query_row_block, preferred_element_type=jnp.float32)
        * score_scale
    )
    value_gradient = jnp.einsum(
        "gik,igd->kd", weights_low, gradient_rows, preferred_element_type=jnp.float32
    )
    return (query_portion, jnp.concatenate([key_gradient, value_gradient], axis=1))


def trunk_allowed(trunk_mask, offset, key_count, branch_len):
    tokens = offset + jnp.arange(key_count, dtype=jnp.int32)
    blocks = jnp.arange(trunk_mask.shape[1], dtype=jnp.int32)
    onehot = (tokens[None, :] // BLK == blocks[:, None]).astype(jnp.float32)
    visible = jnp.dot(trunk_mask, onehot, preferred_element_type=jnp.float32) > 0.5
    spread = jnp.broadcast_to(visible[:, None, :], (visible.shape[0], BLK, key_count))
    return spread.reshape(branch_len, key_count)


def branch_allowed(branch_mask, branch_len):
    block_count = branch_mask.shape[0]
    spread = jnp.broadcast_to(
        branch_mask[:, None, :, None] > 0, (block_count, BLK, block_count, BLK)
    ).reshape(branch_len, branch_len)
    position = jnp.arange(branch_len, dtype=jnp.int32)
    query_block = position[:, None] // BLK
    key_block = position[None, :] // BLK
    earlier = (key_block < query_block) & spread
    causal = (key_block == query_block) & (position[None, :] <= position[:, None])
    return earlier | causal


def shards(
    queries,
    branch_keys,
    branch_value_rows,
    trunk_key_rows,
    trunk_value_rows,
    attn_out,
    out_grad,
    block_mask,
):
    branch_len = queries.shape[1]
    group_width = queries.shape[2] // HEAD_WIDTH
    score_scale = 1.0 / math.sqrt(HEAD_WIDTH)
    query_row_block = queries[0].reshape(branch_len, group_width, HEAD_WIDTH)
    gradient_rows = out_grad[0].reshape(branch_len, group_width, HEAD_WIDTH)
    output_rows = attn_out[0].reshape(branch_len, group_width, HEAD_WIDTH)
    branch_own_keys = branch_keys[0]
    branch_own_values = branch_value_rows[0]
    mask_rows = block_mask[0]
    query_blocks = branch_len // BLK
    trunk_blocks = mask_rows.shape[1] - query_blocks
    trunk_mask = mask_rows[:, :trunk_blocks].astype(jnp.float32)
    own_allowed = branch_allowed(mask_rows[:, trunk_blocks:], branch_len)
    own_scores = jnp.where(
        own_allowed[None], head_scores(query_row_block, branch_own_keys, score_scale), masked_fill
    )
    row_max = jnp.max(own_scores, axis=2, keepdims=True)
    row_total = jnp.sum(jnp.exp(own_scores - row_max), axis=2, keepdims=True)
    trunk_rows, trunk_vals = (
        lax.all_gather(trunk_key_rows, "ctx", axis=0, tiled=True),
        lax.all_gather(trunk_value_rows, "ctx", axis=0, tiled=True),
    )
    trunk_len = trunk_rows.shape[0]
    block_len = math.gcd(512, trunk_len)
    block_total = trunk_len // block_len
    key_blocks = trunk_rows.reshape(block_total, block_len, HEAD_WIDTH)
    value_blocks = trunk_vals.reshape(block_total, block_len, HEAD_WIDTH)
    offsets = jnp.arange(block_total, dtype=jnp.int32) * block_len

    def stats_step(running, inputs):
        run_max, run_total = running
        key_block, offset = inputs
        allowed = trunk_allowed(trunk_mask, offset, block_len, branch_len)
        scores = jnp.where(
            allowed[None], head_scores(query_row_block, key_block, score_scale), masked_fill
        )
        new_max = jnp.maximum(run_max, jnp.max(scores, axis=2, keepdims=True))
        new_total = run_total * jnp.exp(run_max - new_max) + jnp.sum(
            jnp.exp(scores - new_max), axis=2, keepdims=True
        )
        return ((new_max, new_total), None)

    (row_max, row_total), ignored = lax.scan(
        stats_step, (row_max, row_total), (key_blocks, offsets)
    )
    log_total = row_max + jnp.log(row_total)
    out_dot = jnp.sum(
        gradient_rows.astype(jnp.float32) * output_rows.astype(jnp.float32), axis=2
    ).T[:, :, None]
    own_query, own_grad = block_gradients(
        query_row_block,
        gradient_rows,
        branch_own_keys,
        branch_own_values,
        own_allowed,
        log_total,
        out_dot,
        score_scale,
    )

    def grad_step(query_sum, inputs):
        key_block, value_block, offset = inputs
        allowed = trunk_allowed(trunk_mask, offset, block_len, branch_len)
        query_portion, key_value_pair = block_gradients(
            query_row_block,
            gradient_rows,
            key_block,
            value_block,
            allowed,
            log_total,
            out_dot,
            score_scale,
        )
        return (query_sum + query_portion, key_value_pair)

    query_sum, trunk_grad = lax.scan(grad_step, own_query, (key_blocks, value_blocks, offsets))
    query_out = (
        (query_sum * score_scale)
        .astype(jnp.bfloat16)
        .reshape(1, branch_len, group_width * HEAD_WIDTH)
    )
    branch_out = own_grad.astype(jnp.bfloat16)[None]
    trunk_term = lax.optimization_barrier(
        trunk_grad.reshape(trunk_len, 2 * HEAD_WIDTH).astype(jnp.bfloat16)
    ).astype(jnp.float32)
    reduced = lax.psum_scatter(
        trunk_term.astype(jnp.bfloat16), "ctx", scatter_dimension=0, tiled=True
    )
    trunk_out = lax.psum_scatter(reduced, "branch", scatter_dimension=0, tiled=True).astype(
        jnp.float32
    )
    return (query_out, branch_out, trunk_out.astype(jnp.bfloat16))


def solution(mesh):
    ctx, branch = mesh.shape["ctx"], mesh.shape["branch"]

    def body(queries, *rest):
        trunk_part = rest[2].shape[0]
        paired = (
            ctx == 2
            and branch & (branch - 1) == 0
            and queries.shape[0] == 1
            and queries.shape[1] == BLK
            and trunk_part % (8 * branch) == 0
            and trunk_part <= 1024
        )
        return (paired_shards if paired else shards)(queries, *rest)

    return jax.shard_map(
        body,
        mesh=mesh,
        in_specs=(
            P(("ctx", "branch"), None, "head"),
            P(("ctx", "branch"), None, "head"),
            P(("ctx", "branch"), None, "head"),
            P("ctx", "head"),
            P("ctx", "head"),
            P(("ctx", "branch"), None, "head"),
            P(("ctx", "branch"), None, "head"),
            P(("ctx", "branch"), None, None),
        ),
        out_specs=(
            P(("ctx", "branch"), None, "head"),
            P(("ctx", "branch"), None, "head"),
            P(("ctx", "branch"), "head"),
        ),
        check_vma=False,
    )
```

```python
import functools
import math

import jax
import jax.numpy as jnp
from jax import lax
from jax.experimental import pallas as pl
from jax.experimental.pallas import tpu as pltpu
from jax.sharding import PartitionSpec as P

HEAD_WIDTH = 128
BLK = 128


masked_fill = -1e30
VMEM = pl.BlockSpec(memory_space=pltpu.VMEM)
HBM = pl.BlockSpec(memory_space=pltpu.HBM)
SMEM = pl.BlockSpec(memory_space=pltpu.SMEM)
LOG2_E = 1.4426950408889634
NT = (((1,), (1,)), ((), ()))
TN = (((0,), (0,)), ((), ()))


def mm(a, b, dims=(((1,), (0,)), ((), ()))):
    return lax.dot_general(a, b, dims, preferred_element_type=jnp.float32)


def stacked(ref, chunk, heads):
    return jnp.concatenate(
        [
            ref[0, :, j * HEAD_WIDTH : (j + 1) * HEAD_WIDTH]
            for j in range(chunk * heads, (chunk + 1) * heads)
        ],
        axis=0,
    )


def trunk_bias(mask_ref, part, shape, trunk_blocks):
    token = part * shape[0] + lax.broadcasted_iota(jnp.int32, shape, 0)
    visible = jnp.zeros(shape, jnp.int32)
    for block in range(trunk_blocks):
        inside = (token >= block * BLK) & (token < (block + 1) * BLK)
        visible = jnp.where(inside, mask_ref[0, 0, block], visible)
    return jnp.where(visible > 0, 0.0, masked_fill)


def pack_kernel(tk_ref, tv_ref, kv_ref, sems):
    count = tk_ref.shape[0]
    copies = [
        pltpu.make_async_copy(tk_ref, kv_ref.at[:count], sems.at[0]),
        pltpu.make_async_copy(tv_ref, kv_ref.at[count:], sems.at[1]),
    ]
    for copy in copies:
        copy.start()
    for copy in copies:
        copy.wait()


def own_kernel(
    trunk_blocks,
    heads,
    part_ref,
    mask_in,
    q_in,
    g_in,
    o_in,
    bk_in,
    bv_in,
    tk_in,
    tv_in,
    q_ref,
    g_ref,
    keys_ref,
    e_ref,
    gs_ref,
    stat_ref,
    bias_ref,
    o_ref,
    values_ref,
    mask_ref,
    sems,
):
    rows = q_ref.shape[1]
    own = bk_in.shape[1]
    count = tk_in.shape[0]
    width = heads * rows
    scale = LOG2_E / math.sqrt(HEAD_WIDTH)
    chunks = q_ref.shape[2] // (heads * HEAD_WIDTH)
    pairs = [
        (mask_in, mask_ref),
        (bk_in.at[0], keys_ref.at[:own]),
        (tk_in, keys_ref.at[own:]),
        (q_in, q_ref),
        (bv_in.at[0], values_ref.at[:own]),
        (tv_in, values_ref.at[own:]),
        (g_in, g_ref),
        (o_in, o_ref),
    ]
    copies = [pltpu.make_async_copy(a, b, sems.at[i]) for i, (a, b) in enumerate(pairs)]
    for copy in copies:
        copy.start()
    key_row = lax.broadcasted_iota(jnp.int32, (own, rows), 0)
    query_row = lax.broadcasted_iota(jnp.int32, (own, rows), 1)
    causal = jnp.where(key_row <= query_row, 0.0, masked_fill)
    ones = jnp.ones((8, HEAD_WIDTH), jnp.bfloat16)
    for copy in copies[:4]:
        copy.wait()
    bias_ref[...] = trunk_bias(mask_ref, 1 - part_ref[0], (count, rows), trunk_blocks)
    bias = trunk_bias(mask_ref, part_ref[0], (count, rows), trunk_blocks)
    bias = jnp.concatenate([jnp.concatenate([causal, bias], axis=0)] * heads, axis=1)
    keys = keys_ref[...]
    for chunk in range(chunks):
        at = slice(chunk * width, (chunk + 1) * width)
        q = stacked(q_ref, chunk, heads)
        s = mm(keys, q, NT) * scale + bias
        top = jnp.max(s, axis=0, keepdims=True)
        e = jnp.exp2(s - top)
        e_ref[:, at] = e
        stat_ref[0:8, at] = jnp.broadcast_to(top, (8, width))
        stat_ref[8:16, at] = jnp.broadcast_to(jnp.sum(e, axis=0, keepdims=True), (8, width))
    for copy in copies[4:]:
        copy.wait()
    values = values_ref[...]
    for chunk in range(chunks):
        at = slice(chunk * width, (chunk + 1) * width)
        g = stacked(g_ref, chunk, heads)
        prod = g.astype(jnp.float32) * stacked(o_ref, chunk, heads).astype(jnp.float32)
        high = prod.astype(jnp.bfloat16)
        low = (prod - high.astype(jnp.float32)).astype(jnp.bfloat16)
        dot = mm(ones, high, NT) + mm(ones, low, NT)
        gs_ref[:, at] = e_ref[:, at] * (mm(values, g, NT) - dot[:1])
        stat_ref[16:24, at] = dot


def far_kernel(
    heads,
    q_ref,
    g_ref,
    kv_ref,
    stat_ref,
    bias_ref,
    pair_ref,
    ds_ref,
    factor_ref,
):
    rows = q_ref.shape[1]
    count = kv_ref.shape[0] // 2
    scale = 1.0 / math.sqrt(HEAD_WIDTH)
    keys = kv_ref[:count]
    values = kv_ref[count:]
    width = heads * rows
    bias = jnp.concatenate([bias_ref[...]] * heads, axis=1)
    dk = jnp.zeros((count, HEAD_WIDTH), jnp.float32)
    dv = jnp.zeros((count, HEAD_WIDTH), jnp.float32)
    for chunk in range(q_ref.shape[2] // (heads * HEAD_WIDTH)):
        at = slice(chunk * width, (chunk + 1) * width)
        q = stacked(q_ref, chunk, heads)
        g = stacked(g_ref, chunk, heads)
        s = mm(keys, q, NT) * (scale * LOG2_E) + bias
        old = stat_ref[0:1, at]
        top = jnp.maximum(old, jnp.max(s, axis=0, keepdims=True))
        e = jnp.exp2(s - top)
        shrink = jnp.exp2(old - top)
        total = stat_ref[8:9, at] * shrink + jnp.sum(e, axis=0, keepdims=True)
        inverse = 1.0 / total
        w = e * inverse
        ds = (w * (mm(values, g, NT) - stat_ref[16:17, at])).astype(jnp.bfloat16)
        dk += mm(ds, q)
        dv += mm(w.astype(jnp.bfloat16), g)
        ds_ref[:, at] = ds
        factor_ref[:, at] = jnp.broadcast_to(shrink * inverse, (8, width))
    pair_ref[:, :HEAD_WIDTH] = (dk * scale).astype(jnp.bfloat16)
    pair_ref[:, HEAD_WIDTH:] = dv.astype(jnp.bfloat16)


def rest_kernel(
    heads,
    q_ref,
    g_ref,
    near_ref,
    kv_ref,
    e_ref,
    gs_ref,
    ds_ref,
    factor_ref,
    dq_ref,
    branch_ref,
    trunk_ref,
):
    rows = q_ref.shape[1]
    count = kv_ref.shape[0] // 2
    own = near_ref.shape[0] - count
    scale = 1.0 / math.sqrt(HEAD_WIDTH)
    keys = jnp.concatenate([near_ref[...], kv_ref[:count]], axis=0)
    width = heads * rows
    dk = jnp.zeros((own + count, HEAD_WIDTH), jnp.float32)
    dv = jnp.zeros((own + count, HEAD_WIDTH), jnp.float32)
    for chunk in range(q_ref.shape[2] // (heads * HEAD_WIDTH)):
        at = slice(chunk * width, (chunk + 1) * width)
        q = stacked(q_ref, chunk, heads)
        g = stacked(g_ref, chunk, heads)
        factor = factor_ref[0:1, at]
        w = (e_ref[:, at] * factor).astype(jnp.bfloat16)
        ds = (gs_ref[:, at] * factor).astype(jnp.bfloat16)
        dk += mm(ds, q)
        dv += mm(w, g)
        dq = mm(keys, jnp.concatenate([ds, ds_ref[:, at]], axis=0), TN) * scale
        for j in range(heads):
            head = chunk * heads + j
            dq_ref[0, :, head * HEAD_WIDTH : (head + 1) * HEAD_WIDTH] = (
                dq[:, j * rows : (j + 1) * rows].T.astype(jnp.bfloat16)
            )
    dk = (dk * scale).astype(jnp.bfloat16)
    dv = dv.astype(jnp.bfloat16)
    branch_ref[0, :, :HEAD_WIDTH] = dk[:own]
    branch_ref[0, :, HEAD_WIDTH:] = dv[:own]
    trunk_ref[:, :HEAD_WIDTH] = dk[own:]
    trunk_ref[:, HEAD_WIDTH:] = dv[own:]


def in_hbm(*arrays):
    return [pltpu.with_memory_space_constraint(array, pltpu.HBM) for array in arrays]


def call(kernel, out_shape, in_specs, flops, bytes_accessed, scratch=()):
    return pl.pallas_call(
        kernel,
        out_shape=out_shape,
        in_specs=in_specs,
        out_specs=[VMEM] * len(out_shape),
        scratch_shapes=scratch,
        cost_estimate=pl.CostEstimate(
            flops=flops, bytes_accessed=bytes_accessed, transcendentals=0
        ),
        compiler_params=pltpu.CompilerParams(vmem_limit_bytes=16 << 20),
    )


def halved(rows, axis, bit):
    size = lax.axis_size(axis)
    mine = (lax.axis_index(axis) // bit) % 2
    parts = rows.reshape(2, rows.shape[0] // 2, rows.shape[1])
    other = lax.ppermute(
        lax.dynamic_index_in_dim(parts, 1 - mine, 0, False),
        axis,
        [(i, i ^ bit) for i in range(size)],
    )
    kept = lax.dynamic_index_in_dim(parts, mine, 0, False)
    return (kept.astype(jnp.float32) + other.astype(jnp.float32)).astype(jnp.bfloat16)


def paired_shards(
    queries,
    branch_keys,
    branch_value_rows,
    trunk_key_rows,
    trunk_value_rows,
    attn_out,
    out_grad,
    block_mask,
):
    rows = queries.shape[1]
    group = queries.shape[2] // HEAD_WIDTH
    own = branch_keys.shape[1]
    count = trunk_key_rows.shape[0]
    trunk_blocks = block_mask.shape[2] - rows // BLK
    lanes = group * rows
    heads = group // 2 if group % 2 == 0 else group
    swap = [(0, 1), (1, 0)]
    near = own + count
    mac = 2 * lanes * HEAD_WIDTH
    shape = jax.ShapeDtypeStruct
    packed = call(
        pack_kernel,
        [shape((2 * count, HEAD_WIDTH), jnp.bfloat16)],
        [HBM] * 2,
        0,
        8 * count * HEAD_WIDTH,
        [pltpu.SemaphoreType.DMA((2,))],
    )(*in_hbm(trunk_key_rows, trunk_value_rows))[0]
    far = lax.ppermute(packed, "ctx", swap)
    q, g, near_keys, e, gs, stats, bias = call(
        functools.partial(own_kernel, trunk_blocks, heads),
        [
            shape(queries.shape, jnp.bfloat16),
            shape(queries.shape, jnp.bfloat16),
            shape((near, HEAD_WIDTH), jnp.bfloat16),
            shape((near, lanes), jnp.float32),
            shape((near, lanes), jnp.float32),
            shape((24, lanes), jnp.float32),
            shape((count, rows), jnp.float32),
        ],
        [SMEM] + [HBM] * 8,
        2 * near * mac,
        6 * rows * lanes,
        [
            pltpu.VMEM(queries.shape, jnp.bfloat16),
            pltpu.VMEM((near, HEAD_WIDTH), jnp.bfloat16),
            pltpu.SMEM(block_mask.shape, jnp.int32),
            pltpu.SemaphoreType.DMA((8,)),
        ],
    )(
        lax.axis_index("ctx").astype(jnp.int32).reshape(1),
        *in_hbm(
            block_mask,
            queries,
            out_grad,
            attn_out,
            branch_keys,
            branch_value_rows,
            trunk_key_rows,
            trunk_value_rows,
        ),
    )
    pair, ds, factor = call(
        functools.partial(far_kernel, group),
        [
            shape((count, 2 * HEAD_WIDTH), jnp.bfloat16),
            shape((count, lanes), jnp.bfloat16),
            shape((8, lanes), jnp.float32),
        ],
        [VMEM] * 5,
        4 * count * mac,
        4 * rows * lanes,
    )(q, g, far, stats, bias)
    came = lax.ppermute(pair, "ctx", swap)
    query_out, branch_out, kept = call(
        functools.partial(rest_kernel, group),
        [
            shape(queries.shape, jnp.bfloat16),
            shape((1, own, 2 * HEAD_WIDTH), jnp.bfloat16),
            shape((count, 2 * HEAD_WIDTH), jnp.bfloat16),
        ],
        [VMEM] * 8,
        (3 * near + count) * mac,
        6 * rows * lanes,
    )(q, g, near_keys, far, e, gs, ds, factor)
    total = (kept.astype(jnp.float32) + came.astype(jnp.float32)).astype(jnp.bfloat16)
    bit = lax.axis_size("branch") // 2
    while bit:
        total = halved(total, "branch", bit)
        bit //= 2
    return (query_out, branch_out, total)


def head_scores(query_row_block, key_row_block, score_scale):
    return (
        jnp.einsum(
            "igd,kd->gik", query_row_block, key_row_block, preferred_element_type=jnp.float32
        )
        * score_scale
    )
def block_gradients(
    query_row_block,
    gradient_rows,
    key_row_block,
    value_rows,
    allowed,
    log_total,
    out_dot,
    score_scale,
):
    scores = head_scores(query_row_block, key_row_block, score_scale)
    weights = jnp.exp(jnp.where(allowed[None], scores, masked_fill) - log_total)
    weights_low = weights.astype(jnp.bfloat16)
    grad_weights = jnp.einsum(
        "igd,kd->gik", gradient_rows, value_rows, preferred_element_type=jnp.float32
    )
    grad_scores = (weights * (grad_weights - out_dot)).astype(jnp.bfloat16)
    query_portion = jnp.einsum(
        "gik,kd->igd", grad_scores, key_row_block, preferred_element_type=jnp.float32
    )
    key_gradient = (
        jnp.einsum("gik,igd->kd", grad_scores, query_row_block, preferred_element_type=jnp.float32)
        * score_scale
    )
    value_gradient = jnp.einsum(
        "gik,igd->kd", weights_low, gradient_rows, preferred_element_type=jnp.float32
    )
    return (query_portion, jnp.concatenate([key_gradient, value_gradient], axis=1))


def trunk_allowed(trunk_mask, offset, key_count, branch_len):
    tokens = offset + jnp.arange(key_count, dtype=jnp.int32)
    blocks = jnp.arange(trunk_mask.shape[1], dtype=jnp.int32)
    onehot = (tokens[None, :] // BLK == blocks[:, None]).astype(jnp.float32)
    visible = jnp.dot(trunk_mask, onehot, preferred_element_type=jnp.float32) > 0.5
    spread = jnp.broadcast_to(visible[:, None, :], (visible.shape[0], BLK, key_count))
    return spread.reshape(branch_len, key_count)


def branch_allowed(branch_mask, branch_len):
    block_count = branch_mask.shape[0]
    spread = jnp.broadcast_to(
        branch_mask[:, None, :, None] > 0, (block_count, BLK, block_count, BLK)
    ).reshape(branch_len, branch_len)
    position = jnp.arange(branch_len, dtype=jnp.int32)
    query_block = position[:, None] // BLK
    key_block = position[None, :] // BLK
    earlier = (key_block < query_block) & spread
    causal = (key_block == query_block) & (position[None, :] <= position[:, None])
    return earlier | causal


def shards(
    queries,
    branch_keys,
    branch_value_rows,
    trunk_key_rows,
    trunk_value_rows,
    attn_out,
    out_grad,
    block_mask,
):
    branch_len = queries.shape[1]
    group_width = queries.shape[2] // HEAD_WIDTH
    score_scale = 1.0 / math.sqrt(HEAD_WIDTH)
    query_row_block = queries[0].reshape(branch_len, group_width, HEAD_WIDTH)
    gradient_rows = out_grad[0].reshape(branch_len, group_width, HEAD_WIDTH)
    output_rows = attn_out[0].reshape(branch_len, group_width, HEAD_WIDTH)
    branch_own_keys = branch_keys[0]
    branch_own_values = branch_value_rows[0]
    mask_rows = block_mask[0]
    query_blocks = branch_len // BLK
    trunk_blocks = mask_rows.shape[1] - query_blocks
    trunk_mask = mask_rows[:, :trunk_blocks].astype(jnp.float32)
    own_allowed = branch_allowed(mask_rows[:, trunk_blocks:], branch_len)
    own_scores = jnp.where(
        own_allowed[None], head_scores(query_row_block, branch_own_keys, score_scale), masked_fill
    )
    row_max = jnp.max(own_scores, axis=2, keepdims=True)
    row_total = jnp.sum(jnp.exp(own_scores - row_max), axis=2, keepdims=True)
    trunk_rows, trunk_vals = (
        lax.all_gather(trunk_key_rows, "ctx", axis=0, tiled=True),
        lax.all_gather(trunk_value_rows, "ctx", axis=0, tiled=True),
    )
    trunk_len = trunk_rows.shape[0]
    block_len = math.gcd(512, trunk_len)
    block_total = trunk_len // block_len
    key_blocks = trunk_rows.reshape(block_total, block_len, HEAD_WIDTH)
    value_blocks = trunk_vals.reshape(block_total, block_len, HEAD_WIDTH)
    offsets = jnp.arange(block_total, dtype=jnp.int32) * block_len

    def stats_step(running, inputs):
        run_max, run_total = running
        key_block, offset = inputs
        allowed = trunk_allowed(trunk_mask, offset, block_len, branch_len)
        scores = jnp.where(
            allowed[None], head_scores(query_row_block, key_block, score_scale), masked_fill
        )
        new_max = jnp.maximum(run_max, jnp.max(scores, axis=2, keepdims=True))
        new_total = run_total * jnp.exp(run_max - new_max) + jnp.sum(
            jnp.exp(scores - new_max), axis=2, keepdims=True
        )
        return ((new_max, new_total), None)

    (row_max, row_total), ignored = lax.scan(
        stats_step, (row_max, row_total), (key_blocks, offsets)
    )
    log_total = row_max + jnp.log(row_total)
    out_dot = jnp.sum(
        gradient_rows.astype(jnp.float32) * output_rows.astype(jnp.float32), axis=2
    ).T[:, :, None]
    own_query, own_grad = block_gradients(
        query_row_block,
        gradient_rows,
        branch_own_keys,
        branch_own_values,
        own_allowed,
        log_total,
        out_dot,
        score_scale,
    )

    def grad_step(query_sum, inputs):
        key_block, value_block, offset = inputs
        allowed = trunk_allowed(trunk_mask, offset, block_len, branch_len)
        query_portion, key_value_pair = block_gradients(
            query_row_block,
            gradient_rows,
            key_block,
            value_block,
            allowed,
            log_total,
            out_dot,
            score_scale,
        )
        return (query_sum + query_portion, key_value_pair)

    query_sum, trunk_grad = lax.scan(grad_step, own_query, (key_blocks, value_blocks, offsets))
    query_out = (
        (query_sum * score_scale)
        .astype(jnp.bfloat16)
        .reshape(1, branch_len, group_width * HEAD_WIDTH)
    )
    branch_out = own_grad.astype(jnp.bfloat16)[None]
    trunk_term = lax.optimization_barrier(
        trunk_grad.reshape(trunk_len, 2 * HEAD_WIDTH).astype(jnp.bfloat16)
    ).astype(jnp.float32)
    reduced = lax.psum_scatter(
        trunk_term.astype(jnp.bfloat16), "ctx", scatter_dimension=0, tiled=True
    )
    trunk_out = lax.psum_scatter(reduced, "branch", scatter_dimension=0, tiled=True).astype(
        jnp.float32
    )
    return (query_out, branch_out, trunk_out.astype(jnp.bfloat16))


def solution(mesh):
    ctx, branch = mesh.shape["ctx"], mesh.shape["branch"]

    def body(queries, *rest):
        trunk_part = rest[2].shape[0]
        paired = (
            ctx == 2
            and branch & (branch - 1) == 0
            and queries.shape[0] == 1
            and queries.shape[1] == BLK
            and trunk_part % (8 * branch) == 0
            and trunk_part <= 1024
        )
        return (paired_shards if paired else shards)(queries, *rest)

    return jax.shard_map(
        body,
        mesh=mesh,
        in_specs=(
            P(("ctx", "branch"), None, "head"),
            P(("ctx", "branch"), None, "head"),
            P(("ctx", "branch"), None, "head"),
            P("ctx", "head"),
            P("ctx", "head"),
            P(("ctx", "branch"), None, "head"),
            P(("ctx", "branch"), None, "head"),
            P(("ctx", "branch"), None, None),
        ),
        out_specs=(
            P(("ctx", "branch"), None, "head"),
            P(("ctx", "branch"), None, "head"),
            P(("ctx", "branch"), "head"),
        ),
        check_vma=False,
    )
```

```python
import functools
import math

import jax
import jax.numpy as jnp
from jax import lax
from jax.experimental import pallas as pl
from jax.experimental.pallas import tpu as pltpu
from jax.sharding import PartitionSpec as P

HEAD_WIDTH = 128
BLK = 128


masked_fill = -1e30
VMEM = pl.BlockSpec(memory_space=pltpu.VMEM)
HBM = pl.BlockSpec(memory_space=pltpu.HBM)
SMEM = pl.BlockSpec(memory_space=pltpu.SMEM)
LOG2_E = 1.4426950408889634
NT = (((1,), (1,)), ((), ()))
TN = (((0,), (0,)), ((), ()))


def mm(a, b, dims=(((1,), (0,)), ((), ()))):
    return lax.dot_general(a, b, dims, preferred_element_type=jnp.float32)


def stacked(ref, chunk, heads):
    return jnp.concatenate(
        [
            ref[0, :, j * HEAD_WIDTH : (j + 1) * HEAD_WIDTH]
            for j in range(chunk * heads, (chunk + 1) * heads)
        ],
        axis=0,
    )


def trunk_bias(mask_ref, part, shape, trunk_blocks):
    token = part * shape[0] + lax.broadcasted_iota(jnp.int32, shape, 0)
    visible = jnp.zeros(shape, jnp.int32)
    for block in range(trunk_blocks):
        inside = (token >= block * BLK) & (token < (block + 1) * BLK)
        visible = jnp.where(inside, mask_ref[0, 0, block], visible)
    return jnp.where(visible > 0, 0.0, masked_fill)


def pack_kernel(tk_ref, tv_ref, kv_ref, sems):
    count = tk_ref.shape[0]
    copies = [
        pltpu.make_async_copy(tk_ref, kv_ref.at[:count], sems.at[0]),
        pltpu.make_async_copy(tv_ref, kv_ref.at[count:], sems.at[1]),
    ]
    for copy in copies:
        copy.start()
    for copy in copies:
        copy.wait()


def own_kernel(
    trunk_blocks,
    heads,
    part_ref,
    mask_in,
    q_in,
    g_in,
    o_in,
    bk_in,
    bv_in,
    tk_in,
    tv_in,
    q_ref,
    g_ref,
    keys_ref,
    e_ref,
    gs_ref,
    stat_ref,
    bias_ref,
    o_ref,
    values_ref,
    mask_ref,
    sems,
):
    rows = q_ref.shape[1]
    own = bk_in.shape[1]
    count = tk_in.shape[0]
    width = heads * rows
    scale = LOG2_E / math.sqrt(HEAD_WIDTH)
    chunks = q_ref.shape[2] // (heads * HEAD_WIDTH)
    pairs = [
        (mask_in, mask_ref),
        (bk_in.at[0], keys_ref.at[:own]),
        (tk_in, keys_ref.at[own:]),
        (q_in, q_ref),
        (bv_in.at[0], values_ref.at[:own]),
        (tv_in, values_ref.at[own:]),
        (g_in, g_ref),
        (o_in, o_ref),
    ]
    copies = [pltpu.make_async_copy(a, b, sems.at[i]) for i, (a, b) in enumerate(pairs)]
    for copy in copies:
        copy.start()
    key_row = lax.broadcasted_iota(jnp.int32, (own, rows), 0)
    query_row = lax.broadcasted_iota(jnp.int32, (own, rows), 1)
    causal = jnp.where(key_row <= query_row, 0.0, masked_fill)
    ones = jnp.ones((8, HEAD_WIDTH), jnp.bfloat16)
    for copy in copies[:4]:
        copy.wait()
    bias_ref[...] = trunk_bias(mask_ref, 1 - part_ref[0], (count, rows), trunk_blocks)
    bias = trunk_bias(mask_ref, part_ref[0], (count, rows), trunk_blocks)
    bias = jnp.concatenate([jnp.concatenate([causal, bias], axis=0)] * heads, axis=1)
    keys = keys_ref[...]
    for chunk in range(chunks):
        at = slice(chunk * width, (chunk + 1) * width)
        q = stacked(q_ref, chunk, heads)
        s = mm(keys, q, NT) * scale + bias
        top = jnp.max(s, axis=0, keepdims=True)
        e = jnp.exp2(s - top)
        e_ref[:, at] = e
        stat_ref[0:8, at] = jnp.broadcast_to(top, (8, width))
        stat_ref[8:16, at] = jnp.broadcast_to(jnp.sum(e, axis=0, keepdims=True), (8, width))
    for copy in copies[4:]:
        copy.wait()
    values = values_ref[...]
    for chunk in range(chunks):
        at = slice(chunk * width, (chunk + 1) * width)
        g = stacked(g_ref, chunk, heads)
        prod = g.astype(jnp.float32) * stacked(o_ref, chunk, heads).astype(jnp.float32)
        high = prod.astype(jnp.bfloat16)
        low = (prod - high.astype(jnp.float32)).astype(jnp.bfloat16)
        dot = mm(ones, high, NT) + mm(ones, low, NT)
        gs_ref[:, at] = e_ref[:, at] * (mm(values, g, NT) - dot[:1])
        stat_ref[16:24, at] = dot


def far_kernel(
    heads,
    q_ref,
    g_ref,
    kv_ref,
    stat_ref,
    bias_ref,
    pair_ref,
    ds_ref,
    factor_ref,
):
    rows = q_ref.shape[1]
    count = kv_ref.shape[0] // 2
    scale = 1.0 / math.sqrt(HEAD_WIDTH)
    keys = kv_ref[:count]
    values = kv_ref[count:]
    width = heads * rows
    bias = jnp.concatenate([bias_ref[...]] * heads, axis=1)
    dk = jnp.zeros((count, HEAD_WIDTH), jnp.float32)
    dv = jnp.zeros((count, HEAD_WIDTH), jnp.float32)
    for chunk in range(q_ref.shape[2] // (heads * HEAD_WIDTH)):
        at = slice(chunk * width, (chunk + 1) * width)
        q = stacked(q_ref, chunk, heads)
        g = stacked(g_ref, chunk, heads)
        s = mm(keys, q, NT) * (scale * LOG2_E) + bias
        old = stat_ref[0:1, at]
        top = jnp.maximum(old, jnp.max(s, axis=0, keepdims=True))
        e = jnp.exp2(s - top)
        shrink = jnp.exp2(old - top)
        total = stat_ref[8:9, at] * shrink + jnp.sum(e, axis=0, keepdims=True)
        inverse = 1.0 / total
        w = e * inverse
        ds = (w * (mm(values, g, NT) - stat_ref[16:17, at])).astype(jnp.bfloat16)
        dk += mm(ds, q)
        dv += mm(w.astype(jnp.bfloat16), g)
        ds_ref[:, at] = ds
        factor_ref[:, at] = jnp.broadcast_to(shrink * inverse, (8, width))
    pair_ref[:, :HEAD_WIDTH] = (dk * scale).astype(jnp.bfloat16)
    pair_ref[:, HEAD_WIDTH:] = dv.astype(jnp.bfloat16)


def rest_kernel(
    heads,
    q_ref,
    g_ref,
    near_ref,
    kv_ref,
    e_ref,
    gs_ref,
    ds_ref,
    factor_ref,
    dq_ref,
    branch_ref,
    trunk_ref,
):
    rows = q_ref.shape[1]
    count = kv_ref.shape[0] // 2
    own = near_ref.shape[0] - count
    scale = 1.0 / math.sqrt(HEAD_WIDTH)
    keys = jnp.concatenate([near_ref[...], kv_ref[:count]], axis=0)
    width = heads * rows
    dk = jnp.zeros((own + count, HEAD_WIDTH), jnp.float32)
    dv = jnp.zeros((own + count, HEAD_WIDTH), jnp.float32)
    for chunk in range(q_ref.shape[2] // (heads * HEAD_WIDTH)):
        at = slice(chunk * width, (chunk + 1) * width)
        q = stacked(q_ref, chunk, heads)
        g = stacked(g_ref, chunk, heads)
        factor = factor_ref[0:1, at]
        w = (e_ref[:, at] * factor).astype(jnp.bfloat16)
        ds = (gs_ref[:, at] * factor).astype(jnp.bfloat16)
        dk += mm(ds, q)
        dv += mm(w, g)
        dq = mm(keys, jnp.concatenate([ds, ds_ref[:, at]], axis=0), TN) * scale
        for j in range(heads):
            head = chunk * heads + j
            dq_ref[0, :, head * HEAD_WIDTH : (head + 1) * HEAD_WIDTH] = (
                dq[:, j * rows : (j + 1) * rows].T.astype(jnp.bfloat16)
            )
    dk = (dk * scale).astype(jnp.bfloat16)
    dv = dv.astype(jnp.bfloat16)
    branch_ref[0, :, :HEAD_WIDTH] = dk[:own]
    branch_ref[0, :, HEAD_WIDTH:] = dv[:own]
    trunk_ref[:, :HEAD_WIDTH] = dk[own:]
    trunk_ref[:, HEAD_WIDTH:] = dv[own:]


def in_hbm(*arrays):
    return [pltpu.with_memory_space_constraint(array, pltpu.HBM) for array in arrays]


def call(kernel, out_shape, in_specs, flops, bytes_accessed, scratch=()):
    return pl.pallas_call(
        kernel,
        out_shape=out_shape,
        in_specs=in_specs,
        out_specs=[VMEM] * len(out_shape),
        scratch_shapes=scratch,
        cost_estimate=pl.CostEstimate(
            flops=flops, bytes_accessed=bytes_accessed, transcendentals=0
        ),
        compiler_params=pltpu.CompilerParams(vmem_limit_bytes=16 << 20),
    )


def halved(rows, bit, crossed):
    size, heads = lax.axis_size("branch"), lax.axis_size("head")
    mine = (lax.axis_index("branch") // bit) % 2
    parts = rows.reshape(2, rows.shape[0] // 2, rows.shape[1])
    other = lax.ppermute(
        lax.dynamic_index_in_dim(parts, 1 - mine, 0, False),
        ("branch", "head"),
        [
            (i * heads + h, (i ^ bit) * heads + (h ^ crossed))
            for i in range(size)
            for h in range(heads)
        ],
    )
    kept = lax.dynamic_index_in_dim(parts, mine, 0, False)
    if crossed:
        kept = lax.ppermute(kept, "head", [(h, h ^ 1) for h in range(heads)])
    return (kept.astype(jnp.float32) + other.astype(jnp.float32)).astype(jnp.bfloat16)


def paired_shards(
    queries,
    branch_keys,
    branch_value_rows,
    trunk_key_rows,
    trunk_value_rows,
    attn_out,
    out_grad,
    block_mask,
):
    rows = queries.shape[1]
    group = queries.shape[2] // HEAD_WIDTH
    own = branch_keys.shape[1]
    count = trunk_key_rows.shape[0]
    trunk_blocks = block_mask.shape[2] - rows // BLK
    lanes = group * rows
    heads = group // 2 if group % 2 == 0 else group
    swap = [(0, 1), (1, 0)]
    near = own + count
    mac = 2 * lanes * HEAD_WIDTH
    shape = jax.ShapeDtypeStruct
    packed = call(
        pack_kernel,
        [shape((2 * count, HEAD_WIDTH), jnp.bfloat16)],
        [HBM] * 2,
        0,
        8 * count * HEAD_WIDTH,
        [pltpu.SemaphoreType.DMA((2,))],
    )(*in_hbm(trunk_key_rows, trunk_value_rows))[0]
    far = lax.ppermute(packed, "ctx", swap)
    q, g, near_keys, e, gs, stats, bias = call(
        functools.partial(own_kernel, trunk_blocks, heads),
        [
            shape(queries.shape, jnp.bfloat16),
            shape(queries.shape, jnp.bfloat16),
            shape((near, HEAD_WIDTH), jnp.bfloat16),
            shape((near, lanes), jnp.float32),
            shape((near, lanes), jnp.float32),
            shape((24, lanes), jnp.float32),
            shape((count, rows), jnp.float32),
        ],
        [SMEM] + [HBM] * 8,
        2 * near * mac,
        6 * rows * lanes,
        [
            pltpu.VMEM(queries.shape, jnp.bfloat16),
            pltpu.VMEM((near, HEAD_WIDTH), jnp.bfloat16),
            pltpu.SMEM(block_mask.shape, jnp.int32),
            pltpu.SemaphoreType.DMA((8,)),
        ],
    )(
        lax.axis_index("ctx").astype(jnp.int32).reshape(1),
        *in_hbm(
            block_mask,
            queries,
            out_grad,
            attn_out,
            branch_keys,
            branch_value_rows,
            trunk_key_rows,
            trunk_value_rows,
        ),
    )
    pair, ds, factor = call(
        functools.partial(far_kernel, group),
        [
            shape((count, 2 * HEAD_WIDTH), jnp.bfloat16),
            shape((count, lanes), jnp.bfloat16),
            shape((8, lanes), jnp.float32),
        ],
        [VMEM] * 5,
        4 * count * mac,
        4 * rows * lanes,
    )(q, g, far, stats, bias)
    came = lax.ppermute(pair, "ctx", swap)
    query_out, branch_out, kept = call(
        functools.partial(rest_kernel, group),
        [
            shape(queries.shape, jnp.bfloat16),
            shape((1, own, 2 * HEAD_WIDTH), jnp.bfloat16),
            shape((count, 2 * HEAD_WIDTH), jnp.bfloat16),
        ],
        [VMEM] * 8,
        (3 * near + count) * mac,
        6 * rows * lanes,
    )(q, g, near_keys, far, e, gs, ds, factor)
    total = (kept.astype(jnp.float32) + came.astype(jnp.float32)).astype(jnp.bfloat16)
    steps = lax.axis_size("branch").bit_length() - 1
    crossings = steps // 2 * 2 if lax.axis_size("head") % 2 == 0 else 0
    for step in range(steps):
        total = halved(total, 1 << (steps - 1 - step), int(step < crossings))
    return (query_out, branch_out, total)


def head_scores(query_row_block, key_row_block, score_scale):
    return (
        jnp.einsum(
            "igd,kd->gik", query_row_block, key_row_block, preferred_element_type=jnp.float32
        )
        * score_scale
    )
def block_gradients(
    query_row_block,
    gradient_rows,
    key_row_block,
    value_rows,
    allowed,
    log_total,
    out_dot,
    score_scale,
):
    scores = head_scores(query_row_block, key_row_block, score_scale)
    weights = jnp.exp(jnp.where(allowed[None], scores, masked_fill) - log_total)
    weights_low = weights.astype(jnp.bfloat16)
    grad_weights = jnp.einsum(
        "igd,kd->gik", gradient_rows, value_rows, preferred_element_type=jnp.float32
    )
    grad_scores = (weights * (grad_weights - out_dot)).astype(jnp.bfloat16)
    query_portion = jnp.einsum(
        "gik,kd->igd", grad_scores, key_row_block, preferred_element_type=jnp.float32
    )
    key_gradient = (
        jnp.einsum("gik,igd->kd", grad_scores, query_row_block, preferred_element_type=jnp.float32)
        * score_scale
    )
    value_gradient = jnp.einsum(
        "gik,igd->kd", weights_low, gradient_rows, preferred_element_type=jnp.float32
    )
    return (query_portion, jnp.concatenate([key_gradient, value_gradient], axis=1))


def trunk_allowed(trunk_mask, offset, key_count, branch_len):
    tokens = offset + jnp.arange(key_count, dtype=jnp.int32)
    blocks = jnp.arange(trunk_mask.shape[1], dtype=jnp.int32)
    onehot = (tokens[None, :] // BLK == blocks[:, None]).astype(jnp.float32)
    visible = jnp.dot(trunk_mask, onehot, preferred_element_type=jnp.float32) > 0.5
    spread = jnp.broadcast_to(visible[:, None, :], (visible.shape[0], BLK, key_count))
    return spread.reshape(branch_len, key_count)


def branch_allowed(branch_mask, branch_len):
    block_count = branch_mask.shape[0]
    spread = jnp.broadcast_to(
        branch_mask[:, None, :, None] > 0, (block_count, BLK, block_count, BLK)
    ).reshape(branch_len, branch_len)
    position = jnp.arange(branch_len, dtype=jnp.int32)
    query_block = position[:, None] // BLK
    key_block = position[None, :] // BLK
    earlier = (key_block < query_block) & spread
    causal = (key_block == query_block) & (position[None, :] <= position[:, None])
    return earlier | causal


def shards(
    queries,
    branch_keys,
    branch_value_rows,
    trunk_key_rows,
    trunk_value_rows,
    attn_out,
    out_grad,
    block_mask,
):
    branch_len = queries.shape[1]
    group_width = queries.shape[2] // HEAD_WIDTH
    score_scale = 1.0 / math.sqrt(HEAD_WIDTH)
    query_row_block = queries[0].reshape(branch_len, group_width, HEAD_WIDTH)
    gradient_rows = out_grad[0].reshape(branch_len, group_width, HEAD_WIDTH)
    output_rows = attn_out[0].reshape(branch_len, group_width, HEAD_WIDTH)
    branch_own_keys = branch_keys[0]
    branch_own_values = branch_value_rows[0]
    mask_rows = block_mask[0]
    query_blocks = branch_len // BLK
    trunk_blocks = mask_rows.shape[1] - query_blocks
    trunk_mask = mask_rows[:, :trunk_blocks].astype(jnp.float32)
    own_allowed = branch_allowed(mask_rows[:, trunk_blocks:], branch_len)
    own_scores = jnp.where(
        own_allowed[None], head_scores(query_row_block, branch_own_keys, score_scale), masked_fill
    )
    row_max = jnp.max(own_scores, axis=2, keepdims=True)
    row_total = jnp.sum(jnp.exp(own_scores - row_max), axis=2, keepdims=True)
    trunk_rows, trunk_vals = (
        lax.all_gather(trunk_key_rows, "ctx", axis=0, tiled=True),
        lax.all_gather(trunk_value_rows, "ctx", axis=0, tiled=True),
    )
    trunk_len = trunk_rows.shape[0]
    block_len = math.gcd(512, trunk_len)
    block_total = trunk_len // block_len
    key_blocks = trunk_rows.reshape(block_total, block_len, HEAD_WIDTH)
    value_blocks = trunk_vals.reshape(block_total, block_len, HEAD_WIDTH)
    offsets = jnp.arange(block_total, dtype=jnp.int32) * block_len

    def stats_step(running, inputs):
        run_max, run_total = running
        key_block, offset = inputs
        allowed = trunk_allowed(trunk_mask, offset, block_len, branch_len)
        scores = jnp.where(
            allowed[None], head_scores(query_row_block, key_block, score_scale), masked_fill
        )
        new_max = jnp.maximum(run_max, jnp.max(scores, axis=2, keepdims=True))
        new_total = run_total * jnp.exp(run_max - new_max) + jnp.sum(
            jnp.exp(scores - new_max), axis=2, keepdims=True
        )
        return ((new_max, new_total), None)

    (row_max, row_total), ignored = lax.scan(
        stats_step, (row_max, row_total), (key_blocks, offsets)
    )
    log_total = row_max + jnp.log(row_total)
    out_dot = jnp.sum(
        gradient_rows.astype(jnp.float32) * output_rows.astype(jnp.float32), axis=2
    ).T[:, :, None]
    own_query, own_grad = block_gradients(
        query_row_block,
        gradient_rows,
        branch_own_keys,
        branch_own_values,
        own_allowed,
        log_total,
        out_dot,
        score_scale,
    )

    def grad_step(query_sum, inputs):
        key_block, value_block, offset = inputs
        allowed = trunk_allowed(trunk_mask, offset, block_len, branch_len)
        query_portion, key_value_pair = block_gradients(
            query_row_block,
            gradient_rows,
            key_block,
            value_block,
            allowed,
            log_total,
            out_dot,
            score_scale,
        )
        return (query_sum + query_portion, key_value_pair)

    query_sum, trunk_grad = lax.scan(grad_step, own_query, (key_blocks, value_blocks, offsets))
    query_out = (
        (query_sum * score_scale)
        .astype(jnp.bfloat16)
        .reshape(1, branch_len, group_width * HEAD_WIDTH)
    )
    branch_out = own_grad.astype(jnp.bfloat16)[None]
    trunk_term = lax.optimization_barrier(
        trunk_grad.reshape(trunk_len, 2 * HEAD_WIDTH).astype(jnp.bfloat16)
    ).astype(jnp.float32)
    reduced = lax.psum_scatter(
        trunk_term.astype(jnp.bfloat16), "ctx", scatter_dimension=0, tiled=True
    )
    trunk_out = lax.psum_scatter(reduced, "branch", scatter_dimension=0, tiled=True).astype(
        jnp.float32
    )
    return (query_out, branch_out, trunk_out.astype(jnp.bfloat16))


def solution(mesh):
    ctx, branch = mesh.shape["ctx"], mesh.shape["branch"]

    def body(queries, *rest):
        trunk_part = rest[2].shape[0]
        paired = (
            ctx == 2
            and branch & (branch - 1) == 0
            and queries.shape[0] == 1
            and queries.shape[1] == BLK
            and trunk_part % (8 * branch) == 0
            and trunk_part <= 1024
        )
        return (paired_shards if paired else shards)(queries, *rest)

    return jax.shard_map(
        body,
        mesh=mesh,
        in_specs=(
            P(("ctx", "branch"), None, "head"),
            P(("ctx", "branch"), None, "head"),
            P(("ctx", "branch"), None, "head"),
            P("ctx", "head"),
            P("ctx", "head"),
            P(("ctx", "branch"), None, "head"),
            P(("ctx", "branch"), None, "head"),
            P(("ctx", "branch"), None, None),
        ),
        out_specs=(
            P(("ctx", "branch"), None, "head"),
            P(("ctx", "branch"), None, "head"),
            P(("ctx", "branch"), "head"),
        ),
        check_vma=False,
    )
```
